32 devices in a mesh: fsdp: 16 (over z, y, x), replica: 2 (over core).
Axes of the slice: x: 2, y: 2, z: 4, core: 2. Of those that a mesh axis runs over, the one named last changes fastest.
Arguments:
- inputs: bfloat16 [4096, 1024], P(('fsdp', 'replica')), may hold values from -6 to 6
- cotangent: bfloat16 [4096, 1024], P(('fsdp', 'replica')), may hold values from -6 to 6
- attn_gain: bfloat16 [1024], P('fsdp'), may hold values from 0.5 to 1.5
- attn_shift: bfloat16 [1024], P('fsdp'), may hold values from -3 to 3
- qkv_weight: bfloat16 [1024, 3072], P('fsdp'), as said below
- qkv_bias: bfloat16 [3072], P('fsdp'), may hold values from -3 to 3
- proj_weight: bfloat16 [1024, 1024], P('fsdp'), may hold values from -1 to 1
- proj_bias: bfloat16 [1024], P('fsdp'), may hold values from -3 to 3
- mlp_gain: bfloat16 [1024], P('fsdp'), may hold values from 0.5 to 1.5
- mlp_shift: bfloat16 [1024], P('fsdp'), may hold values from -3 to 3
- up_weight: bfloat16 [1024, 4096], P('fsdp'), may hold values from -0.1875 to 0.1875
- up_bias: bfloat16 [4096], P('fsdp'), may hold values from -3 to 3
- down_weight: bfloat16 [4096, 1024], P('fsdp'), may hold values from -0.09375 to 0.09375
- down_bias: bfloat16 [1024], P('fsdp'), may hold values from -3 to 3
Outputs:
- output: bfloat16 [4096, 1024], P(('fsdp', 'replica'))
- grad_inputs: bfloat16 [4096, 1024], P(('fsdp', 'replica'))
- grad_attn_gain: float32 [1024], P('fsdp')
- grad_attn_shift: float32 [1024], P('fsdp')
- grad_qkv_weight: float32 [1024, 3072], P('fsdp')
- grad_qkv_bias: float32 [3072], P('fsdp')
- grad_proj_weight: float32 [1024, 1024], P('fsdp')
- grad_proj_bias: float32 [1024], P('fsdp')
- grad_mlp_gain: float32 [1024], P('fsdp')
- grad_mlp_shift: float32 [1024], P('fsdp')
- grad_up_weight: float32 [1024, 4096], P('fsdp')
- grad_up_bias: float32 [4096], P('fsdp')
- grad_down_weight: float32 [4096, 1024], P('fsdp')
- grad_down_bias: float32 [1024], P('fsdp')
The draws below stay inside these ranges and needn't reach their ends.
Inputs may be any that keep to these rules, and one draw needn't show every extreme that they name: qkv_weight has entries of order 1024^-0.5 times a few; its draw is a scaled normal law.
All inputs are finite; a program needn't handle non-finite values.
Results may differ from the reference program's by a relative error of at most 0.017.
Values may be sent and summed in bfloat16 or wider, within the bound.
A program may use at most 192 MiB of HBM per device.

```python
import math
import jax
import jax.numpy as jnp
from jax import lax

D = 1024
H = 16
ROT = 16
FF = 4096
SEQ = 128
TOKENS = 4096


def draw_qkv_weight(key, part):
    entries = jnp.clip(jax.random.normal(key, (D, 3 * D), jnp.float32), -6.0, 6.0) * D ** (-0.5)
    return entries.astype(jnp.bfloat16)


def steps_of(key, dims, cuts, smallest, high):
    factor_of, own = 1.0, jax.random.fold_in(key, 6)
    for dim, parts in cuts:
        steps = jnp.exp(jax.random.uniform(jax.random.fold_in(own, dim), (parts,), jnp.float32, smallest / len(cuts), high / len(cuts)))
        factor_of = factor_of * jnp.repeat(steps, dims[dim] // parts).reshape([-1 if axis == dim else 1 for axis in range(len(dims))])
    return factor_of


def noise(stream_key, dims, width, reach, split=(), kind=jnp.bfloat16):
    values = jax.random.normal(stream_key, dims, jnp.float32) * width
    if len(split) > 0:
        values = steps_of(stream_key, dims, split, -0.22, 0.18) * values
    return jnp.clip(values, min=-reach, max=reach).astype(kind)


def setup_inputs(seed: int = 0) -> dict:
    keys = jax.random.split(jax.random.key(seed), 15)
    inputs = noise(keys[0], (TOKENS, D), 1.0, 6.0, ((0, 32),))
    cotangent = noise(keys[1], (TOKENS, D), 1.0, 6.0, ((0, 32),))
    attn_gain = jnp.clip(1.0 + 0.1 * jax.random.normal(keys[2], (D,), jnp.float32), 0.5, 1.5).astype(jnp.bfloat16)
    attn_shift = noise(keys[3], (D,), 0.5, 3.0, ((0, 16),))
    qkv_weight = draw_qkv_weight(jax.random.fold_in(keys[14], 71), 0)
    qkv_bias = noise(keys[5], (3 * D,), 0.5, 3.0, ((0, 16),))
    proj_weight = noise(keys[6], (D, D), (D * 4 // SEQ) ** -0.5, 1.0, ((0, 16),))
    proj_bias = noise(keys[7], (D,), 0.5, 3.0, ((0, 16),))
    mlp_gain = jnp.clip(1.0 + 0.1 * jax.random.normal(keys[8], (D,), jnp.float32), 0.5, 1.5).astype(jnp.bfloat16)
    mlp_shift = noise(keys[9], (D,), 0.5, 3.0, ((0, 16),))
    up_weight = noise(keys[10], (D, FF), D ** -0.5, 0.1875, ((0, 16),))
    up_bias = noise(keys[11], (FF,), 0.5, 3.0, ((0, 16),))
    down_weight = noise(keys[12], (FF, D), FF ** -0.5, 0.09375, ((0, 16),))
    down_bias = noise(keys[13], (D,), 0.5, 3.0, ((0, 16),))
    return dict(inputs=inputs, cotangent=cotangent, attn_gain=attn_gain, attn_shift=attn_shift, qkv_weight=qkv_weight, qkv_bias=qkv_bias, proj_weight=proj_weight, proj_bias=proj_bias, mlp_gain=mlp_gain, mlp_shift=mlp_shift, up_weight=up_weight, up_bias=up_bias, down_weight=down_weight, down_bias=down_bias)


EPSILON = 1e-05
THETA = 10000.0
SQRT_HALF = 0.7071067811865476
INV_ROOT_TAU = 0.3989422804014327

def product(pattern, left_side, right_side):
    return jnp.einsum(pattern, left_side.astype(jnp.float32), right_side.astype(jnp.float32))

def normalize(residual, gain_row, shift_row):
    centered = residual - lax.optimization_barrier(jnp.mean(residual, axis=-1, keepdims=True))
    inverse = lax.rsqrt(lax.optimization_barrier(jnp.mean(centered * centered, axis=-1, keepdims=True)) + EPSILON)
    unit_rows = centered * inverse
    return (unit_rows * gain_row + shift_row, unit_rows, inverse)

def normalize_back(upstream, unit_rows, inverse, gain_row):
    scaled = upstream * gain_row
    grad_rows = inverse * (scaled - lax.optimization_barrier(jnp.mean(scaled, axis=-1, keepdims=True)) - unit_rows * lax.optimization_barrier(jnp.mean(scaled * unit_rows, axis=-1, keepdims=True)))
    return (grad_rows, lax.optimization_barrier(jnp.sum(upstream * unit_rows, axis=0)), lax.optimization_barrier(jnp.sum(upstream, axis=0)))

def rotary_tables():
    half_rot = ROT // 2
    frequency = jnp.exp(jnp.arange(half_rot, dtype=jnp.float32) * (-2.0 * math.log(THETA) / ROT))
    angles = jnp.arange(SEQ, dtype=jnp.float32)[:, None] * frequency[None, :]
    return (jnp.cos(angles), jnp.sin(angles))

def rotate(heads_data, cosine_table, sine_table, inverse_turn):
    half_rot = ROT // 2
    first_half = heads_data[..., :half_rot]
    second_half = heads_data[..., half_rot:ROT]
    passive = heads_data[..., ROT:]
    cosine_part = cosine_table[None, :, None, :]
    sine_part = sine_table[None, :, None, :]
    if inverse_turn:
        sine_part = -sine_part
    return jnp.concatenate([first_half * cosine_part - second_half * sine_part, second_half * cosine_part + first_half * sine_part, passive], axis=-1)

def gelu_slope(pre_act):
    return 0.5 * (1.0 + lax.erf(pre_act * SQRT_HALF)) + pre_act * jnp.exp(-0.5 * pre_act * pre_act) * INV_ROOT_TAU

def masked_scores(queries, keys_rot):
    head_dim = queries.shape[-1]
    scores = product('bqhd,bkhd->bhqk', queries, keys_rot) * head_dim ** (-0.5)
    positions = jnp.arange(SEQ)
    causal = positions[:, None] >= positions[None, :]
    return jnp.where(causal[None, None], scores, -jnp.inf)

def forward_pass(inputs, forward_set):
    attn_gain, attn_shift, qkv_weight, qkv_bias, proj_weight, proj_bias, mlp_gain, mlp_shift, up_weight, up_bias, down_weight, down_bias = forward_set
    row_count, features = inputs.shape
    seq_count = row_count // SEQ
    head_dim = features // H
    residual = inputs.astype(jnp.float32)
    normed, attn_unit, attn_inverse = normalize(residual, attn_gain.astype(jnp.float32), attn_shift.astype(jnp.float32))
    attn_in = normed.astype(jnp.bfloat16)
    projected = jnp.dot(attn_in, qkv_weight, preferred_element_type=jnp.float32) + qkv_bias.astype(jnp.float32)
    shaped = projected.reshape(seq_count, SEQ, 3, H, head_dim)
    cosine_table, sine_table = rotary_tables()
    queries = rotate(shaped[:, :, 0], cosine_table, sine_table, False).astype(jnp.bfloat16)
    keys_rot = rotate(shaped[:, :, 1], cosine_table, sine_table, False).astype(jnp.bfloat16)
    values = shaped[:, :, 2].astype(jnp.bfloat16)
    scores = masked_scores(queries, keys_rot)
    peak_score = lax.optimization_barrier(jnp.max(scores, axis=-1, keepdims=True))
    logsum = peak_score + jnp.log(lax.optimization_barrier(jnp.sum(jnp.exp(scores - peak_score), axis=-1, keepdims=True)))
    weights = jnp.exp(scores - logsum).astype(jnp.bfloat16)
    context = product('bhqk,bkhd->bqhd', weights, values).reshape(row_count, features).astype(jnp.bfloat16)
    attn_out = jnp.dot(context, proj_weight, preferred_element_type=jnp.float32) + proj_bias.astype(jnp.float32)
    normed_mlp, mlp_unit, mlp_inverse = normalize(residual, mlp_gain.astype(jnp.float32), mlp_shift.astype(jnp.float32))
    mlp_in = normed_mlp.astype(jnp.bfloat16)
    pre_act = jnp.dot(mlp_in, up_weight, preferred_element_type=jnp.float32) + up_bias.astype(jnp.float32)
    activated = jax.nn.gelu(pre_act, approximate=False).astype(jnp.bfloat16)
    mlp_out = jnp.dot(activated, down_weight, preferred_element_type=jnp.float32) + down_bias.astype(jnp.float32)
    output = (residual + attn_out + mlp_out).astype(jnp.bfloat16)
    saved = (attn_unit, attn_inverse, attn_in, queries, keys_rot, values, logsum, context, mlp_unit, mlp_inverse, mlp_in, pre_act, activated)
    return (output, saved)

def backward_pass(cotangent, saved, backward_set):
    attn_gain, attn_shift, qkv_weight, qkv_bias, proj_weight, proj_bias, mlp_gain, mlp_shift, up_weight, up_bias, down_weight, down_bias = backward_set
    attn_unit, attn_inverse, attn_in, queries, keys_rot, values, logsum, context, mlp_unit, mlp_inverse, mlp_in, pre_act, activated = saved
    row_count, features = cotangent.shape
    head_dim = features // H
    upstream = cotangent.astype(jnp.float32)
    grad_out_bias = lax.optimization_barrier(jnp.sum(upstream, axis=0))
    grad_down_weight = jnp.dot(activated.T, cotangent, preferred_element_type=jnp.float32)
    grad_pre = jnp.dot(cotangent, down_weight.T, preferred_element_type=jnp.float32) * gelu_slope(pre_act)
    grad_up_bias = lax.optimization_barrier(jnp.sum(grad_pre, axis=0))
    grad_pre_b = grad_pre.astype(jnp.bfloat16)
    grad_up_weight = jnp.dot(mlp_in.T, grad_pre_b, preferred_element_type=jnp.float32)
    grad_mlp_in = jnp.dot(grad_pre_b, up_weight.T, preferred_element_type=jnp.float32)
    grad_proj_weight = jnp.dot(context.T, cotangent, preferred_element_type=jnp.float32)
    grad_context = jnp.dot(cotangent, proj_weight.T, preferred_element_type=jnp.float32).astype(jnp.bfloat16)
    grad_context = grad_context.reshape(queries.shape)
    probs = jnp.exp(masked_scores(queries, keys_rot) - logsum)
    weights = probs.astype(jnp.bfloat16)
    grad_probs = product('bqhd,bkhd->bhqk', grad_context, values)
    grad_values = product('bhqk,bqhd->bkhd', weights, grad_context)
    grad_scores = (probs * (grad_probs - lax.optimization_barrier(jnp.sum(probs * grad_probs, axis=-1, keepdims=True))) * head_dim ** (-0.5)).astype(jnp.bfloat16)
    grad_queries = product('bhqk,bkhd->bqhd', grad_scores, keys_rot)
    grad_keys = product('bhqk,bqhd->bkhd', grad_scores, queries)
    cosine_table, sine_table = rotary_tables()
    grad_projected = jnp.stack([rotate(grad_queries, cosine_table, sine_table, True), rotate(grad_keys, cosine_table, sine_table, True), grad_values], axis=2).reshape(row_count, 3 * features)
    grad_qkv_bias = lax.optimization_barrier(jnp.sum(grad_projected, axis=0))
    grad_projected_b = grad_projected.astype(jnp.bfloat16)
    grad_qkv_weight = jnp.dot(attn_in.T, grad_projected_b, preferred_element_type=jnp.float32)
    grad_attn_in = jnp.dot(grad_projected_b, qkv_weight.T, preferred_element_type=jnp.float32)
    attn_rows, grad_attn_gain, grad_attn_shift = normalize_back(grad_attn_in, attn_unit, attn_inverse, attn_gain.astype(jnp.float32))
    mlp_rows, grad_mlp_gain, grad_mlp_shift = normalize_back(grad_mlp_in, mlp_unit, mlp_inverse, mlp_gain.astype(jnp.float32))
    grad_inputs = (upstream + attn_rows + mlp_rows).astype(jnp.bfloat16)
    gradients = (grad_attn_gain, grad_attn_shift, grad_qkv_weight, grad_qkv_bias, grad_proj_weight, grad_out_bias, grad_mlp_gain, grad_mlp_shift, grad_up_weight, grad_up_bias, grad_down_weight, grad_out_bias)
    return (grad_inputs, gradients)

def reference(inputs, cotangent, attn_gain, attn_shift, qkv_weight, qkv_bias, proj_weight, proj_bias, mlp_gain, mlp_shift, up_weight, up_bias, down_weight, down_bias):
    parameters = (attn_gain, attn_shift, qkv_weight, qkv_bias, proj_weight, proj_bias, mlp_gain, mlp_shift, up_weight, up_bias, down_weight, down_bias)
    block_seqs = math.gcd(TOKENS // SEQ, max(1, 4096 // SEQ))
    block_rows = block_seqs * SEQ
    block_count = TOKENS // block_rows
    input_blocks = inputs.reshape(block_count, block_rows, D)
    cotangent_blocks = cotangent.reshape(block_count, block_rows, D)
    zero_sums = tuple((jnp.zeros(item.shape, jnp.float32) for item in parameters))

    def accumulate(running, block_pair):
        output_block, saved = forward_pass(block_pair[0], parameters)
        grad_block, gradients = backward_pass(block_pair[1], saved, parameters)
        return (tuple((left_sum + right_sum for left_sum, right_sum in zip(running, gradients))), (output_block, grad_block))
    totals, (outputs, grads_in) = lax.scan(accumulate, zero_sums, (input_blocks, cotangent_blocks))
    return (outputs.reshape(TOKENS, D), grads_in.reshape(TOKENS, D), totals[0], totals[1], totals[2], totals[3], totals[4], totals[5], totals[6], totals[7], totals[8], totals[9], totals[10], totals[11])
```

```python
import math

import jax
import jax.numpy as jnp
from jax import lax
from jax.sharding import PartitionSpec as P

H = 16
ROT = 16
SEQ = 128


EPSILON = 1e-05
THETA = 10000.0
SQRT_HALF = 0.7071067811865476
INV_ROOT_TAU = 0.3989422804014327


def product(pattern, left_side, right_side):
    return jnp.einsum(pattern, left_side, right_side, preferred_element_type=jnp.float32)


def normalize(residual, gain_row, shift_row):
    centered = residual - jnp.mean(residual, axis=-1, keepdims=True)
    inverse = lax.rsqrt(jnp.mean(centered * centered, axis=-1, keepdims=True) + EPSILON)
    unit_rows = centered * inverse
    return (unit_rows * gain_row + shift_row, unit_rows, inverse)


def normalize_back(upstream, unit_rows, inverse, gain_row):
    scaled = upstream * gain_row
    grad_rows = inverse * (
        scaled
        - jnp.mean(scaled, axis=-1, keepdims=True)
        - unit_rows * jnp.mean(scaled * unit_rows, axis=-1, keepdims=True)
    )
    return (grad_rows, jnp.sum(upstream * unit_rows, axis=0), jnp.sum(upstream, axis=0))


def rotary_tables():
    half_rot = ROT // 2
    frequency = jnp.exp(jnp.arange(half_rot, dtype=jnp.float32) * (-2.0 * math.log(THETA) / ROT))
    angles = jnp.arange(SEQ, dtype=jnp.float32)[:, None] * frequency[None, :]
    return (jnp.cos(angles), jnp.sin(angles))


def rotate(heads_data, cosine_table, sine_table, inverse_turn):
    half_rot = ROT // 2
    first_half = heads_data[..., :half_rot]
    second_half = heads_data[..., half_rot:ROT]
    passive = heads_data[..., ROT:]
    cosine_part = cosine_table[None, :, None, :]
    sine_part = sine_table[None, :, None, :]
    if inverse_turn:
        sine_part = -sine_part
    return jnp.concatenate(
        [
            first_half * cosine_part - second_half * sine_part,
            second_half * cosine_part + first_half * sine_part,
            passive,
        ],
        axis=-1,
    )


def gelu_slope(pre_act):
    return (
        0.5 * (1.0 + lax.erf(pre_act * SQRT_HALF))
        + pre_act * jnp.exp(-0.5 * pre_act * pre_act) * INV_ROOT_TAU
    )


def masked_scores(queries, keys_rot):
    head_dim = queries.shape[-1]
    scores = product("bqhd,bkhd->bhqk", queries, keys_rot) * head_dim ** (-0.5)
    positions = jnp.arange(SEQ)
    causal = positions[:, None] >= positions[None, :]
    return jnp.where(causal[None, None], scores, -jnp.inf)


ROW_TILE = 16


def partner(x):
    count = lax.axis_size("replica")
    return lax.ppermute(x, "replica", [(i, i ^ 1) for i in range(count)])


def parity():
    return lax.rem(lax.axis_index("replica"), 2)


def own_half(x):
    half = x.shape[-1] // 2
    return lax.dynamic_slice_in_dim(x, parity() * half, half, x.ndim - 1)


def other_half(x):
    half = x.shape[-1] // 2
    return lax.dynamic_slice_in_dim(x, (1 - parity()) * half, half, x.ndim - 1)


def pair_gather(rows):
    return jnp.concatenate([rows, partner(rows)], axis=0)


def pair_halves(rows):
    return jnp.concatenate([own_half(rows), partner(other_half(rows))], axis=0)


def fold(matrix, width):
    return [matrix[:, k : k + width] for k in range(0, matrix.shape[1], width)]


def apply_blocks(rows, blocks):
    parts = [jnp.dot(rows, block, preferred_element_type=jnp.float32) for block in blocks]
    return parts[0] if len(parts) == 1 else jnp.concatenate(parts, axis=-1)


def apply_blocks_back(rows, blocks):
    pieces = fold(rows, rows.shape[1] // len(blocks))
    total = None
    for piece, block in zip(pieces, blocks):
        part = jnp.dot(piece, block.T, preferred_element_type=jnp.float32)
        total = part if total is None else total + part
    return total


def pad_rows(flat, width):
    tile = ROW_TILE * width
    size = flat.shape[-1]
    padded = -(-size // tile) * tile
    widths = [(0, 0)] * (flat.ndim - 1) + [(0, padded - size)]
    return jnp.pad(flat, widths).reshape(flat.shape[:-1] + (padded // width, width))


def gather_all(matrices, vectors):
    width = min(m.shape[1] for m in matrices)
    packed = []
    for matrix in matrices:
        packed.extend(fold(matrix, width))
    packed.append(pad_rows(jnp.concatenate(vectors), width))
    full = lax.all_gather(jnp.concatenate(packed, axis=0), "fsdp", axis=0, tiled=False)
    start = 0
    whole = []
    for matrix in matrices:
        blocks = []
        for _ in range(matrix.shape[1] // width):
            blocks.append(full[:, start : start + matrix.shape[0]].reshape(-1, width))
            start += matrix.shape[0]
        whole.append(blocks)
    tail = full[:, start:].reshape(full.shape[0], -1)
    rows = []
    start = 0
    for vector in vectors:
        rows.append(tail[:, start : start + vector.shape[0]].reshape(-1))
        start += vector.shape[0]
    return (whole, rows)


def weight_grad(left_pair, right_pair, width):
    return [
        jnp.dot(left_pair.T, block, preferred_element_type=jnp.float32).astype(jnp.bfloat16)
        for block in fold(right_pair, width)
    ]


def scatter_all(block_lists, vectors):
    owners = lax.axis_size("fsdp")
    width = block_lists[0][0].shape[1]
    sums = jnp.concatenate([v.reshape(owners, -1) for v in vectors], axis=1)
    sums = sums + partner(sums)
    packed = [b.reshape(owners, -1, width) for blocks in block_lists for b in blocks]
    packed.append(pad_rows(sums, width).astype(jnp.bfloat16))
    owned = lax.psum_scatter(
        jnp.concatenate(packed, axis=1), "fsdp", scatter_dimension=0, tiled=False
    )
    distance = 2
    if distance < lax.axis_size("replica"):
        owned = owned.astype(jnp.float32)
    while distance < lax.axis_size("replica"):
        count = lax.axis_size("replica")
        moved = lax.ppermute(owned, "replica", [(i, i ^ distance) for i in range(count)])
        owned = owned + moved
        distance *= 2
    main = sum(p.shape[1] for p in packed[:-1])
    other = partner(owned[:main])
    first = parity() == 0
    left = jnp.where(first, owned[:main], other)
    right = jnp.where(first, other, owned[:main])
    start = 0
    whole = []
    for blocks in block_lists:
        rows = blocks[0].shape[0] // owners
        stop = start + rows * len(blocks)
        pieces = [side[k : k + rows] for side in (left, right) for k in range(start, stop, rows)]
        whole.append(jnp.concatenate(pieces, axis=1).astype(jnp.float32))
        start = stop
    tail = owned[main:].reshape(-1).astype(jnp.float32)
    totals = []
    start = 0
    for vector in vectors:
        size = vector.shape[0] // owners
        totals.append(tail[start : start + size])
        start += size
    return (whole, totals)


def forward_pass(inputs, forward_set):
    (
        attn_gain,
        attn_shift,
        qkv_weight,
        qkv_bias,
        proj_weight,
        proj_bias,
        mlp_gain,
        mlp_shift,
        up_weight,
        up_bias,
        down_weight,
        down_bias,
    ) = forward_set
    row_count, features = inputs.shape
    seq_count = row_count // SEQ
    head_dim = features // H
    residual = inputs.astype(jnp.float32)
    normed, attn_unit, attn_inverse = normalize(
        residual, attn_gain.astype(jnp.float32), attn_shift.astype(jnp.float32)
    )
    attn_in = normed.astype(jnp.bfloat16)
    projected = apply_blocks(attn_in, qkv_weight) + qkv_bias.astype(
        jnp.float32
    )
    shaped = projected.reshape(seq_count, SEQ, 3, H, head_dim)
    cosine_table, sine_table = rotary_tables()
    queries = rotate(shaped[:, :, 0], cosine_table, sine_table, False).astype(jnp.bfloat16)
    keys_rot = rotate(shaped[:, :, 1], cosine_table, sine_table, False).astype(jnp.bfloat16)
    values = shaped[:, :, 2].astype(jnp.bfloat16)
    scores = masked_scores(queries, keys_rot)
    peak_score = jnp.max(scores, axis=-1, keepdims=True)
    logsum = peak_score + jnp.log(jnp.sum(jnp.exp(scores - peak_score), axis=-1, keepdims=True))
    weights = jnp.exp(scores - logsum).astype(jnp.bfloat16)
    context = (
        product("bhqk,bkhd->bqhd", weights, values)
        .reshape(row_count, features)
        .astype(jnp.bfloat16)
    )
    attn_out = apply_blocks(context, proj_weight) + proj_bias.astype(
        jnp.float32
    )
    normed_mlp, mlp_unit, mlp_inverse = normalize(
        residual, mlp_gain.astype(jnp.float32), mlp_shift.astype(jnp.float32)
    )
    mlp_in = normed_mlp.astype(jnp.bfloat16)
    pre_act = apply_blocks(mlp_in, up_weight) + up_bias.astype(
        jnp.float32
    )
    activated = jax.nn.gelu(pre_act, approximate=False).astype(jnp.bfloat16)
    mlp_out = apply_blocks(activated, down_weight) + down_bias.astype(jnp.float32)
    output = (residual + attn_out + mlp_out).astype(jnp.bfloat16)
    saved = (
        attn_unit,
        attn_inverse,
        attn_in,
        queries,
        keys_rot,
        values,
        logsum,
        context,
        mlp_unit,
        mlp_inverse,
        mlp_in,
        pre_act,
        activated,
    )
    return (output, saved)


def backward_pass(cotangent, saved, backward_set):
    (
        attn_gain,
        attn_shift,
        qkv_weight,
        qkv_bias,
        proj_weight,
        proj_bias,
        mlp_gain,
        mlp_shift,
        up_weight,
        up_bias,
        down_weight,
        down_bias,
    ) = backward_set
    (
        attn_unit,
        attn_inverse,
        attn_in,
        queries,
        keys_rot,
        values,
        logsum,
        context,
        mlp_unit,
        mlp_inverse,
        mlp_in,
        pre_act,
        activated,
    ) = saved
    row_count, features = cotangent.shape
    head_dim = features // H
    upstream = cotangent.astype(jnp.float32)
    grad_out_bias = jnp.sum(upstream, axis=0)
    cotangent_pair = pair_halves(cotangent)
    half = features // 2
    grad_down_weight = weight_grad(pair_gather(activated), cotangent_pair, half)
    grad_pre = apply_blocks_back(cotangent, down_weight) * gelu_slope(
        pre_act
    )
    grad_up_bias = jnp.sum(grad_pre, axis=0)
    grad_pre_b = grad_pre.astype(jnp.bfloat16)
    grad_up_weight = weight_grad(pair_gather(mlp_in), pair_halves(grad_pre_b), half)
    grad_mlp_in = apply_blocks_back(grad_pre_b, up_weight)
    grad_proj_weight = weight_grad(pair_gather(context), cotangent_pair, half)
    grad_context = apply_blocks_back(cotangent, proj_weight).astype(
        jnp.bfloat16
    )
    grad_context = grad_context.reshape(queries.shape)
    probs = jnp.exp(masked_scores(queries, keys_rot) - logsum)
    weights = probs.astype(jnp.bfloat16)
    grad_probs = product("bqhd,bkhd->bhqk", grad_context, values)
    grad_values = product("bhqk,bqhd->bkhd", weights, grad_context)
    grad_scores = (
        probs
        * (grad_probs - jnp.sum(probs * grad_probs, axis=-1, keepdims=True))
        * head_dim ** (-0.5)
    ).astype(jnp.bfloat16)
    grad_queries = product("bhqk,bkhd->bqhd", grad_scores, keys_rot)
    grad_keys = product("bhqk,bqhd->bkhd", grad_scores, queries)
    cosine_table, sine_table = rotary_tables()
    grad_projected = jnp.stack(
        [
            rotate(grad_queries, cosine_table, sine_table, True),
            rotate(grad_keys, cosine_table, sine_table, True),
            grad_values,
        ],
        axis=2,
    ).reshape(row_count, 3 * features)
    grad_qkv_bias = jnp.sum(grad_projected, axis=0)
    grad_projected_b = grad_projected.astype(jnp.bfloat16)
    grad_qkv_weight = weight_grad(pair_gather(attn_in), pair_halves(grad_projected_b), half)
    grad_attn_in = apply_blocks_back(grad_projected_b, qkv_weight)
    attn_rows, grad_attn_gain, grad_attn_shift = normalize_back(
        grad_attn_in, attn_unit, attn_inverse, attn_gain.astype(jnp.float32)
    )
    mlp_rows, grad_mlp_gain, grad_mlp_shift = normalize_back(
        grad_mlp_in, mlp_unit, mlp_inverse, mlp_gain.astype(jnp.float32)
    )
    grad_inputs = (upstream + attn_rows + mlp_rows).astype(jnp.bfloat16)
    gradients = (
        grad_attn_gain,
        grad_attn_shift,
        grad_qkv_weight,
        grad_qkv_bias,
        grad_proj_weight,
        grad_out_bias,
        grad_mlp_gain,
        grad_mlp_shift,
        grad_up_weight,
        grad_up_bias,
        grad_down_weight,
        grad_out_bias,
    )
    return (grad_inputs, gradients)


def local(
    inputs,
    cotangent,
    attn_gain,
    attn_shift,
    qkv_weight,
    qkv_bias,
    proj_weight,
    proj_bias,
    mlp_gain,
    mlp_shift,
    up_weight,
    up_bias,
    down_weight,
    down_bias,
):
    weights, vectors = gather_all(
        (qkv_weight, proj_weight, up_weight, down_weight),
        (
            attn_gain,
            attn_shift,
            qkv_bias,
            proj_bias,
            mlp_gain,
            mlp_shift,
            up_bias,
            down_bias,
        ),
    )
    forward_set = (
        vectors[0],
        vectors[1],
        weights[0],
        vectors[2],
        weights[1],
        vectors[3],
        vectors[4],
        vectors[5],
        weights[2],
        vectors[6],
        weights[3],
        vectors[7],
    )
    output, saved = forward_pass(inputs, forward_set)
    grad_inputs, gradients = backward_pass(cotangent, saved, forward_set)
    matrices, rows = scatter_all(
        (gradients[2], gradients[4], gradients[8], gradients[10]),
        (
            gradients[0],
            gradients[1],
            gradients[3],
            gradients[5],
            gradients[6],
            gradients[7],
            gradients[9],
        ),
    )
    totals = (
        rows[0],
        rows[1],
        matrices[0],
        rows[2],
        matrices[1],
        rows[3],
        rows[4],
        rows[5],
        matrices[2],
        rows[6],
        matrices[3],
        rows[3],
    )
    return (
        output,
        grad_inputs,
        totals[0],
        totals[1],
        totals[2],
        totals[3],
        totals[4],
        totals[5],
        totals[6],
        totals[7],
        totals[8],
        totals[9],
        totals[10],
        totals[11],
    )


def solution(mesh):
    return jax.shard_map(
        local,
        mesh=mesh,
        in_specs=(
            P(("fsdp", "replica"), None),
            P(("fsdp", "replica"), None),
            P("fsdp"),
            P("fsdp"),
            P("fsdp", None),
            P("fsdp"),
            P("fsdp", None),
            P("fsdp"),
            P("fsdp"),
            P("fsdp"),
            P("fsdp", None),
            P("fsdp"),
            P("fsdp", None),
            P("fsdp"),
        ),
        out_specs=(
            P(("fsdp", "replica"), None),
            P(("fsdp", "replica"), None),
            P("fsdp"),
            P("fsdp"),
            P("fsdp", None),
            P("fsdp"),
            P("fsdp", None),
            P("fsdp"),
            P("fsdp"),
            P("fsdp"),
            P("fsdp", None),
            P("fsdp"),
            P("fsdp", None),
            P("fsdp"),
        ),
        check_vma=False,
    )
```
